128 devices in a mesh: sect: 2 (over y_lo), op: 64 (over x, y_hi, z, core).
Axes of the slice: x: 4, y: 4 (y_hi: 2, y_lo: 2; y = y_hi * 2 + y_lo), z: 4, core: 2. Of those that a mesh axis runs over, the one named last changes fastest.
Arguments:
- wave: bfloat16 [2, 8192, 256], P('sect', 'op'), may hold values from -6 to 6
- left_ops: bfloat16 [2, 192, 8, 256, 256], P('sect', 'op'), may hold values from -1 to 1
- right_ops: bfloat16 [2, 192, 8, 256, 256], P('sect', 'op'), may hold values from -0.375 to 0.375
- site_ops: float32 [2, 192, 4, 4], P('sect', 'op'), may hold values from -0.21875 to 0.21875
- reach: int32 [2, 192], P('sect', 'op'), may hold values from 1 to 8
- pairing: int32 [2, 8], P('sect'), may hold values from 0 to 7, each once within a row
- site_tensor: bfloat16 [2, 8, 4, 256, 256], P('sect'), may hold values from -0.25 to 0.25
Outputs:
- first_image: bfloat16 [2, 8192, 256], P('sect', 'op')
- second_image: bfloat16 [2, 8192, 256], P('sect', 'op')
- moved_image: bfloat16 [2, 8192, 256], P('sect', 'op')
The draws below stay inside these ranges and needn't reach their ends.
Inputs may be any that keep to these rules, and one draw needn't show every extreme that they name: Each term couples the sectors 0 to reach - 1. `pairing`: each row is a permutation of the 8 sectors.
All inputs are finite; a program needn't handle non-finite values.
Results may differ from the reference program's by a relative error of at most 0.008.
Values may be sent and summed in bfloat16 or wider, within the bound.
No kernel may reach another device: no remote copies, remote signals or barrier semaphores. Data moves between devices by JAX's collectives and lax.ppermute only.
A program may use at most 128 MiB of HBM per device.

```python
import jax
import jax.numpy as jnp
from jax import lax

SECTORS = 8
BLOCK = 256
LOCAL = 4
SECTIONS = 2
TERMS = 192
ROWS = 8192


def plant(result, own_key, least, top_value):
    dims = result.shape
    index_at = [jax.random.randint(jax.random.fold_in(own_key, axis), (), 0, dims[axis]) for axis in range(len(dims))]
    result = result.at[tuple(index_at)].set(least)
    longest = dims.index(max(dims))
    index_at[longest] = (index_at[longest] + 1) % dims[longest]
    return result.at[tuple(index_at)].set(top_value)


def with_spikes(entries, key, source, target, parts, factor):
    def block_of(position):
        return (jnp.arange(entries.shape[position]) // (entries.shape[position] // parts)).reshape((-1,) + (1,) * (entries.ndim - 1 - position))

    one_side = jax.random.permutation(key, parts)[block_of(target)]
    far = (block_of(target) + parts // 2) % parts
    return jnp.where((block_of(source) == one_side) | (block_of(source) == far), factor * entries, entries)


def block_levels(key, shape, shards, smallest, top_value):
    def one(axis_at, parts):
        heights = jax.random.uniform(jax.random.fold_in(jax.random.fold_in(key, 6), axis_at), (parts,), jnp.float32, smallest / len(shards), top_value / len(shards))
        return jnp.repeat(jnp.exp(heights), shape[axis_at] // parts).reshape((-1,) + (1,) * (len(shape) - axis_at - 1))

    factor_of = one(*shards[0])
    for cut in shards[1:]:
        factor_of = factor_of * one(*cut)
    return factor_of


def scatter_about(key, extent, deviation, most, cuts=(), kind=jnp.bfloat16):
    array = deviation * jax.random.normal(key, extent, jnp.float32)
    if cuts:
        array = array * block_levels(key, extent, cuts, -0.22, 0.18)
    return jnp.clip(array, -most, most).astype(kind)


def heavy_noise(stream_key, extent, deviation, most, cuts, heavy, kind=jnp.bfloat16):
    values = deviation * jax.random.normal(stream_key, extent, jnp.float32)
    if cuts:
        values = values * block_levels(stream_key, extent, cuts, -0.22, 0.18)
    return jnp.clip(with_spikes(values, jax.random.fold_in(stream_key, 3), *heavy), -most, most).astype(kind)


def setup_inputs(seed: int = 0) -> dict:
    arg_keys = jax.random.split(jax.random.key(seed), 8)
    return {
        "wave": scatter_about(arg_keys[0], (SECTIONS, ROWS, BLOCK), 1.0, 6.0, ((0, 2), (1, 64))),
        "left_ops": heavy_noise(arg_keys[1], (SECTIONS, TERMS, SECTORS, BLOCK, BLOCK), BLOCK ** -0.5, 1.0, ((0, 2), (1, 64)), (1, 3, 64, 4.0)),
        "right_ops": scatter_about(arg_keys[2], (SECTIONS, TERMS, SECTORS, BLOCK, BLOCK), BLOCK ** -0.5, 0.375, ((0, 2), (1, 64))),
        "site_ops": scatter_about(arg_keys[3], (SECTIONS, TERMS, LOCAL, LOCAL), (LOCAL * TERMS) ** -0.5, 0.21875, ((0, 2), (1, 64)), jnp.float32),
        "reach": plant(jax.random.randint(arg_keys[4], (SECTIONS, TERMS), 1, SECTORS + 1), jax.random.fold_in(arg_keys[4], 1), 1, SECTORS).astype(jnp.int32),
        "pairing": jax.vmap(lambda own: jax.random.permutation(own, SECTORS))(jax.random.split(arg_keys[5], SECTIONS)).reshape((SECTIONS, SECTORS)).astype(jnp.int32),
        "site_tensor": scatter_about(arg_keys[6], (SECTIONS, SECTORS, LOCAL, BLOCK, BLOCK), (2 * BLOCK) ** -0.5, 0.25, ((0, 2),)),
    }


def apply_terms(wave, lefts, rights, mixers, limits, pair):
    sector_ids = jnp.arange(SECTORS, dtype=jnp.int32)
    wave_f = wave.astype(jnp.float32)

    def one_term(total, term):
        left, right, mixer, limit = term
        lifted = jnp.einsum("qab,qsbc->qsac", left.astype(jnp.float32), wave_f).astype(jnp.bfloat16)
        mask = (sector_ids < limit).astype(jnp.float32)
        mixed = jnp.einsum("xy,qyac->qxac", mixer, lifted.astype(jnp.float32), precision=lax.Precision.HIGHEST)
        mixed = (mixed * mask[:, None, None, None]).astype(jnp.bfloat16)
        paired = jnp.take(right, pair, axis=0).astype(jnp.float32)
        return total + jnp.einsum("qsac,qdc->qsad", mixed.astype(jnp.float32), paired), None

    start = jnp.zeros((SECTORS, LOCAL, BLOCK, BLOCK), jnp.float32)
    total, unused = lax.scan(one_term, start, (lefts, rights, mixers, limits))
    return total.astype(jnp.bfloat16)


def renormalize(lefts, tensor, pair):
    onehot = (pair[:, None] == jnp.arange(SECTORS, dtype=jnp.int32)[None, :]).astype(jnp.float32)
    tensor_f = tensor.astype(jnp.float32)

    def one_term(carry, left):
        lifted = jnp.einsum("qab,qsbc->qsac", left.astype(jnp.float32), tensor_f).astype(jnp.bfloat16)
        reduced = jnp.einsum("qsad,qsac->qdc", tensor_f, lifted.astype(jnp.float32)).astype(jnp.bfloat16)
        placed = jnp.einsum("qj,qdc->jdc", onehot, reduced.astype(jnp.float32), precision=lax.Precision.HIGHEST)
        return carry, placed.astype(jnp.bfloat16)

    unused, renewed = lax.scan(one_term, jnp.zeros((), jnp.float32), lefts)
    return renewed


def reference(wave, left_ops, right_ops, site_ops, reach, pairing, site_tensor):
    firsts = []
    seconds = []
    renewed = []
    for section in range(SECTIONS):
        blocks = wave[section].reshape(SECTORS, LOCAL, BLOCK, BLOCK)
        first = apply_terms(blocks, left_ops[section], right_ops[section], site_ops[section], reach[section], pairing[section])
        second = apply_terms(first, left_ops[section], right_ops[section], site_ops[section], reach[section], pairing[section])
        firsts.append(first.reshape(ROWS, BLOCK))
        seconds.append(second.reshape(ROWS, BLOCK))
        renewed.append(renormalize(left_ops[section], site_tensor[section], pairing[section]))
    moved = []
    for section in range(SECTIONS):
        blocks = wave[section].reshape(SECTORS, LOCAL, BLOCK, BLOCK)
        image = apply_terms(blocks, renewed[section - 1], right_ops[section], site_ops[section], reach[section], pairing[section])
        moved.append(image.reshape(ROWS, BLOCK))
    return jnp.stack(firsts), jnp.stack(seconds), jnp.stack(moved)
```

```python
import jax
import jax.numpy as jnp
from jax import lax
from jax.experimental import pallas as pl
from jax.experimental.pallas import tpu as pltpu
from jax.sharding import PartitionSpec as P

NX, NY, NZ, NC = 4, 2, 4, 2
SECTORS = 8
LOCAL = 4
BLOCK = 256
CHUNK = 128
BF16 = jnp.bfloat16
F32 = jnp.float32


def device_at(x, y, z, c):
    return ((x * NY + y) * NZ + z) * NC + c


ALONG_X = [
    [device_at(x, y, z, c) for x in range(NX) for c in range(NC)]
    for y in range(NY)
    for z in range(NZ)
]
ALONG_Z = [
    [device_at(x, y, z, c) for z in range(NZ) for c in range(NC)]
    for x in range(NX)
    for y in range(NY)
]
HOLDERS = [
    [device_at(x, y, (half - x) % NZ, c) for x in range(NX) for y in range(NY)]
    for half in range(SECTORS // NC)
    for c in range(NC)
]
OWNERS = [[q * 8 + k for k in range(8)] for q in range(SECTORS)]
TO_HOLDERS = [(OWNERS[q][k], HOLDERS[q][k]) for q in range(SECTORS) for k in range(8)]
TO_OWNERS = [(HOLDERS[q][k], OWNERS[q][k]) for q in range(SECTORS) for k in range(8)]


def exchange(value, groups):
    return lax.all_to_all(value, "op", 0, 0, axis_index_groups=groups)


def pack_kernel(qx, px, qz, pz, lx, rx, lz, rz, out_x, out_z):
    out_x[0, 0:2] = lx[:, 0]
    out_x[0, 2:4] = rx[:, 0]
    out_z[0, 0:1] = lz[:, 0]
    out_z[0, 1:2] = rz[:, 0]


def pack(lefts, rights, qx, px, qz, pz):
    two = (2, 1, BLOCK, BLOCK)
    one = (1, 1, BLOCK, BLOCK)
    grid_spec = pltpu.PrefetchScalarGridSpec(
        num_scalar_prefetch=4,
        grid=(SECTORS,),
        in_specs=[
            pl.BlockSpec(two, lambda j, qx, px, qz, pz: (0, qx[j], 0, 0)),
            pl.BlockSpec(two, lambda j, qx, px, qz, pz: (0, px[j], 0, 0)),
            pl.BlockSpec(one, lambda j, qx, px, qz, pz: (2, qz[j], 0, 0)),
            pl.BlockSpec(one, lambda j, qx, px, qz, pz: (2, pz[j], 0, 0)),
        ],
        out_specs=[
            pl.BlockSpec((1, 4, BLOCK, BLOCK), lambda j, *_: (j, 0, 0, 0)),
            pl.BlockSpec((1, 2, BLOCK, BLOCK), lambda j, *_: (j, 0, 0, 0)),
        ],
    )
    return pl.pallas_call(
        pack_kernel,
        grid_spec=grid_spec,
        out_shape=[
            jax.ShapeDtypeStruct((SECTORS, 4, BLOCK, BLOCK), BF16),
            jax.ShapeDtypeStruct((SECTORS, 2, BLOCK, BLOCK), BF16),
        ],
        name="pack",
        cost_estimate=pl.CostEstimate(flops=0, bytes_accessed=12 << 20, transcendentals=0),
    )(qx, px, qz, pz, lefts, rights, lefts, rights)


def renew_kernel(slot_x, slot_z, left, tensor, out_x, out_z):
    lefts = left[:, 0].reshape(3 * BLOCK, BLOCK)
    total = [jnp.zeros((BLOCK, BLOCK), F32) for _ in range(3)]
    for s in range(LOCAL):
        site = tensor[0, s]
        lifted = jnp.dot(lefts, site, preferred_element_type=F32).astype(BF16)
        site_t = site.astype(F32).T.astype(BF16)
        for t in range(3):
            total[t] += jnp.dot(
                site_t, lifted[t * BLOCK : (t + 1) * BLOCK], preferred_element_type=F32
            )
    out_x[0, 0] = total[0].astype(BF16)
    out_x[0, 1] = total[1].astype(BF16)
    out_z[0, 0] = total[2].astype(BF16)


def renew(lefts, tensor, slot_x, slot_z):
    grid_spec = pltpu.PrefetchScalarGridSpec(
        num_scalar_prefetch=2,
        grid=(SECTORS,),
        in_specs=[
            pl.BlockSpec((3, 1, BLOCK, BLOCK), lambda q, *_: (0, q, 0, 0)),
            pl.BlockSpec((1, LOCAL, BLOCK, BLOCK), lambda q, *_: (q, 0, 0, 0)),
        ],
        out_specs=[
            pl.BlockSpec((1, 2, BLOCK, BLOCK), lambda q, sx, sz: (sx[q], 0, 0, 0)),
            pl.BlockSpec((1, 1, BLOCK, BLOCK), lambda q, sx, sz: (sz[q], 0, 0, 0)),
        ],
    )
    return pl.pallas_call(
        renew_kernel,
        grid_spec=grid_spec,
        out_shape=[
            jax.ShapeDtypeStruct((SECTORS, 2, BLOCK, BLOCK), BF16),
            jax.ShapeDtypeStruct((SECTORS, 1, BLOCK, BLOCK), BF16),
        ],
        name="renew",
        cost_estimate=pl.CostEstimate(
            flops=24 * 8 * 2 * BLOCK**3, bytes_accessed=10 << 20, transcendentals=0
        ),
    )(slot_x, slot_z, lefts, tensor)


def apply_kernel(mix, left_x, left_z, right_x, right_z, field, out, total):
    step = pl.program_id(0)

    @pl.when(step == 0)
    def _():
        total[...] = jnp.zeros_like(total)

    lefts = [left_x[0, 0], left_x[0, 1], left_z[0, 0]]
    rights = [right_x[0, 0], right_x[0, 1], right_z[0, 0]]
    for t in range(3):
        lifted = [
            jnp.dot(
                lefts[t], field[s * BLOCK : (s + 1) * BLOCK], preferred_element_type=F32
            )
            .astype(BF16)
            .astype(F32)
            for s in range(LOCAL)
        ]
        base = (step * 3 + t) * LOCAL * LOCAL
        for s in range(LOCAL):
            mixed = mix[base + s * LOCAL] * lifted[0]
            for s2 in range(1, LOCAL):
                mixed += mix[base + s * LOCAL + s2] * lifted[s2]
            rows = slice(s * BLOCK, (s + 1) * BLOCK)
            total[rows] += lax.dot_general(
                mixed.astype(BF16),
                rights[t],
                (((1,), (1,)), ((), ())),
                preferred_element_type=F32,
            )

    @pl.when(step == pl.num_programs(0) - 1)
    def _():
        out[...] = total[...].astype(BF16)


def apply_terms(mix, left_x, left_z, right_x, right_z, right_at, field):
    grid_spec = pltpu.PrefetchScalarGridSpec(
        num_scalar_prefetch=1,
        grid=(8,),
        in_specs=[
            pl.BlockSpec((1, 2, BLOCK, BLOCK), lambda j, *_: (j, 0, 0, 0)),
            pl.BlockSpec((1, 1, BLOCK, BLOCK), lambda j, *_: (j, 0, 0, 0)),
            pl.BlockSpec((1, 2, BLOCK, BLOCK), lambda j, *_: (j, right_at, 0, 0)),
            pl.BlockSpec((1, 1, BLOCK, BLOCK), lambda j, *_: (j, right_at, 0, 0)),
            pl.BlockSpec((LOCAL * BLOCK, BLOCK), lambda j, *_: (0, 0)),
        ],
        out_specs=pl.BlockSpec((LOCAL * BLOCK, BLOCK), lambda j, *_: (0, 0)),
        scratch_shapes=[pltpu.VMEM((LOCAL * BLOCK, BLOCK), F32)],
    )
    return pl.pallas_call(
        apply_kernel,
        grid_spec=grid_spec,
        out_shape=jax.ShapeDtypeStruct((LOCAL * BLOCK, BLOCK), BF16),
        name="apply_terms",
        cost_estimate=pl.CostEstimate(
            flops=24 * 8 * 2 * BLOCK**3, bytes_accessed=8 << 20, transcendentals=0
        ),
    )(mix, left_x, left_z, right_x, right_z, field)


def reduce_chunks(partial):
    parts = exchange(partial.reshape(8, CHUNK, BLOCK), HOLDERS)
    return jnp.sum(parts.astype(F32), axis=0).astype(BF16)


def shards(wave, left_ops, right_ops, site_ops, reach, pairing, site_tensor):
    lefts = left_ops[0]
    rights = right_ops[0]
    pair = pairing[0]
    me = lax.axis_index("op")
    x, y, z, c = me // 16, (me // 8) % 2, (me // 2) % 4, me % 2
    sector = ((x + z) % 4) * 2 + c
    slots = jnp.arange(SECTORS, dtype=jnp.int32)
    qx = ((slots // 2 + z) % 4) * 2 + slots % 2
    qz = ((slots // 2 + x) % 4) * 2 + slots % 2
    slot_x = ((pair // 2 - z) % 4) * 2 + pair % 2
    slot_z = ((pair // 2 - x) % 4) * 2 + pair % 2

    packed_x, packed_z = pack(lefts, rights, qx, pair[qx], qz, pair[qz])
    ops_x = exchange(packed_x, ALONG_X)
    ops_z = exchange(packed_z, ALONG_Z)

    mine = jnp.concatenate(
        [site_ops[0].reshape(3, LOCAL * LOCAL), reach[0].astype(F32)[:, None]], axis=1
    )
    table = lax.all_gather(mine, "op", axis=0)
    source_x = device_at(slots // 2, y, z, slots % 2)
    source_z = device_at(x, y, slots // 2, slots % 2)
    rows = jnp.concatenate([table[source_x, 0:2], table[source_z, 2:3]], axis=1)
    mix = rows[:, :, :16] * (sector.astype(F32) < rows[:, :, 16:]).astype(F32)
    mix = mix.reshape(-1)

    sector_rows = lax.all_gather(wave[0], "op", axis=0, tiled=True, axis_index_groups=OWNERS)
    field = lax.ppermute(sector_rows, "op", TO_HOLDERS)

    renewed_x, renewed_z = renew(lefts, site_tensor[0], slot_x, slot_z)
    renewed_x = lax.ppermute(renewed_x, "sect", [(0, 1), (1, 0)])
    renewed_z = lax.ppermute(renewed_z, "sect", [(0, 1), (1, 0)])

    first = reduce_chunks(apply_terms(mix, ops_x, ops_z, ops_x, ops_z, 1, field))
    first_own = lax.ppermute(first, "op", TO_OWNERS)
    first_field = exchange(jnp.broadcast_to(first[None], (8, CHUNK, BLOCK)), HOLDERS)
    first_field = first_field.reshape(LOCAL * BLOCK, BLOCK)
    second = reduce_chunks(apply_terms(mix, ops_x, ops_z, ops_x, ops_z, 1, first_field))
    second_own = lax.ppermute(second, "op", TO_OWNERS)

    moved_x = exchange(renewed_x, ALONG_X)
    moved_z = exchange(renewed_z, ALONG_Z)
    moved = reduce_chunks(apply_terms(mix, moved_x, moved_z, ops_x, ops_z, 1, field))
    moved_own = lax.ppermute(moved, "op", TO_OWNERS)
    return first_own[None], second_own[None], moved_own[None]


def solution(mesh):
    placed = (
        P("sect", "op", None),
        P("sect", "op", None, None, None),
        P("sect", "op", None, None, None),
        P("sect", "op", None, None),
        P("sect", "op"),
        P("sect", None),
        P("sect", None, None, None, None),
    )
    return jax.shard_map(
        shards,
        mesh=mesh,
        in_specs=placed,
        out_specs=(P("sect", "op", None), P("sect", "op", None), P("sect", "op", None)),
        check_vma=False,
    )
```

```python
import functools

import jax
import jax.numpy as jnp
from jax import lax
from jax.experimental import pallas as pl
from jax.experimental.pallas import tpu as pltpu
from jax.sharding import PartitionSpec as P

NX, NY, NZ, NC = 4, 2, 4, 2
DEVICES = NX * NY * NZ * NC
SECTORS = 8
LOCAL = 4
BLOCK = 256
CHUNK = 128
TERMS = 3
STACK = TERMS * BLOCK
MIX_ROWS = 16
ROWS = 2 * STACK + MIX_ROWS
BF16 = jnp.bfloat16
F32 = jnp.float32
ANY = pl.BlockSpec(memory_space=pl.ANY)
SMEM = pl.BlockSpec(memory_space=pltpu.SMEM)
VMEM = pl.BlockSpec(memory_space=pltpu.VMEM)


def device_at(x, y, z, c):
    return (((x % NX) * NY + y) * NZ + z % NZ) * NC + c


PLACES = [
    (x, y, z, c) for x in range(NX) for y in range(NY) for z in range(NZ) for c in range(NC)
]
HOLDERS = [
    [device_at(x, y, half - x, c) for x in range(NX) for y in range(NY)]
    for half in range(SECTORS // NC)
    for c in range(NC)
]
OWNERS = [[q * 8 + k for k in range(8)] for q in range(SECTORS)]
TO_HOLDERS = [(OWNERS[q][k], HOLDERS[q][k]) for q in range(SECTORS) for k in range(8)]
TO_OWNERS = [(HOLDERS[q][k], OWNERS[q][k]) for q in range(SECTORS) for k in range(8)]
LINES = [[device_at(x, y, z, 0) for x in range(NX)] for y in range(NY) for z in range(NZ)]
LINES += [[device_at(x, y, z, 1) for z in range(NZ)] for x in range(NX) for y in range(NY)]


def along(d, flip):
    return [
        (
            device_at(x, y, z, c),
            device_at(x + d * (1 - c), y, z + d * c, c ^ flip),
        )
        for x, y, z, c in PLACES
    ]


def exchange(value, groups):
    return lax.all_to_all(value, "op", 0, 0, axis_index_groups=groups)


def mixer_rows(row, held, sector):
    value = jnp.where(sector < held, row, 0.0)
    high = value.astype(BF16).astype(F32)
    middle = (value - high).astype(BF16).astype(F32)
    low = value - high - middle
    at = lax.broadcasted_iota(jnp.int32, (MIX_ROWS, BLOCK), 0)
    parts = jnp.where(at == 0, high, jnp.where(at == 1, middle, jnp.where(at == 2, low, 0.0)))
    return parts.astype(BF16)


def pack_kernel(place, pair, site, reach, left, right, *refs):
    outs = refs[:5]
    left_buf, right_buf, mix_buf, load_sems, sems = refs[5:]
    x, z, c = place[0], place[1], place[2]
    loads = []
    for t in range(TERMS):
        loads.append(pltpu.make_async_copy(left.at[0, t], left_buf.at[t], load_sems.at[t, 0]))
        loads.append(pltpu.make_async_copy(right.at[0, t], right_buf.at[t], load_sems.at[t, 1]))
    for copy in loads:
        copy.start()
    lane = lax.broadcasted_iota(jnp.int32, (1, BLOCK), 1)
    row = jnp.zeros((1, BLOCK), F32)
    held = jnp.zeros((1, BLOCK), jnp.int32)
    for t in range(TERMS):
        held = jnp.where(lane // 16 == t, reach[t], held)
        for e in range(LOCAL * LOCAL):
            row = jnp.where(lane == t * 16 + e, site[t * 16 + e], row)
    sectors = [lax.rem(i + jnp.where(c == 0, z, x), 4) * 2 + c for i in range(4)]
    sectors += [lax.rem(x + z + d, 4) * 2 + 1 - c for d in range(4)]
    places = [outs[0].at[i] for i in range(4)] + list(outs[1:])
    stores = []

    def store(src, dst):
        stores.append(pltpu.make_async_copy(src, dst, sems.at[len(stores)]))
        stores[-1].start()

    for i, q in enumerate(sectors):
        mix_buf[i] = mixer_rows(row, held, q)
    for i in range(8):
        store(mix_buf.at[i], places[i].at[2 * STACK : ROWS])
    for copy in loads:
        copy.wait()
    for i, q in enumerate(sectors):
        for t in range(TERMS):
            store(left_buf.at[t, q], places[i].at[t * BLOCK : (t + 1) * BLOCK])
            store(right_buf.at[t, pair[q]], places[i].at[STACK + t * BLOCK : STACK + (t + 1) * BLOCK])
    for copy in stores:
        copy.wait()


def pack(place, pair, site, reach, left_ops, right_ops):
    return pl.pallas_call(
        pack_kernel,
        in_specs=[SMEM, SMEM, SMEM, SMEM, ANY, ANY],
        out_specs=[ANY] * 5,
        out_shape=[jax.ShapeDtypeStruct((4, ROWS, BLOCK), BF16)]
        + [jax.ShapeDtypeStruct((ROWS, BLOCK), BF16)] * 4,
        scratch_shapes=[
            pltpu.VMEM((TERMS, SECTORS, BLOCK, BLOCK), BF16),
            pltpu.VMEM((TERMS, SECTORS, BLOCK, BLOCK), BF16),
            pltpu.VMEM((8, MIX_ROWS, BLOCK), BF16),
            pltpu.SemaphoreType.DMA((TERMS, 2)),
            pltpu.SemaphoreType.DMA((56,)),
        ],
        compiler_params=pltpu.CompilerParams(vmem_limit_bytes=56 << 20),
        name="pack",
        cost_estimate=pl.CostEstimate(flops=1 << 20, bytes_accessed=1 << 16, transcendentals=0),
    )(place, pair, site, reach, left_ops, right_ops)


def renew_kernel(place, pair, left, tensor, out):
    lefts = left[0, :, 0].reshape(STACK, BLOCK)
    lifted = []
    sites = []
    for s in range(LOCAL):
        site = tensor[0, 0, s]
        lifted.append(jnp.dot(lefts, site, preferred_element_type=F32).astype(BF16))
        sites.append(site.T)
    sites = jnp.concatenate(sites, axis=1)
    for t in range(TERMS):
        stacked = jnp.concatenate([lifted[s][t * BLOCK : (t + 1) * BLOCK] for s in range(LOCAL)])
        out[0, t] = jnp.dot(sites, stacked, preferred_element_type=F32).astype(BF16)


def renew(kept, place, pair, left_ops, tensor):
    def left_sector(i, place, pair):
        x, z, c = place[0], place[1], place[2]
        wanted = lax.rem(x + z + i, 4) * 2 + (c if kept else 1 - c)
        q = jnp.int32(0)
        for k in range(1, SECTORS):
            q = jnp.where(pair[k] == wanted, k, q)
        return q

    grid_spec = pltpu.PrefetchScalarGridSpec(
        num_scalar_prefetch=2,
        grid=(4,),
        in_specs=[
            pl.BlockSpec((1, TERMS, 1, BLOCK, BLOCK), lambda d, *s: (0, 0, left_sector(d, *s), 0, 0)),
            pl.BlockSpec((1, 1, LOCAL, BLOCK, BLOCK), lambda d, *s: (0, left_sector(d, *s), 0, 0, 0)),
        ],
        out_specs=pl.BlockSpec((1, TERMS, BLOCK, BLOCK), lambda d, *s: (d, 0, 0, 0)),
    )
    return pl.pallas_call(
        renew_kernel,
        grid_spec=grid_spec,
        out_shape=jax.ShapeDtypeStruct((4, TERMS, BLOCK, BLOCK), BF16),
        name="renew_kept" if kept else "renew_swapped",
        cost_estimate=pl.CostEstimate(
            flops=12 * 8 * 2 * BLOCK**3, bytes_accessed=20 << 20, transcendentals=0
        ),
    )(place, pair, left_ops, tensor)


def apply_kernel(groups, renewed, starts, place, field, *refs):
    out, left_buf, right_buf, mix_buf, total, sems = refs[-6:]
    start = refs[-7] if starts else None

    here = jnp.where(place[2] == 0, place[0], place[1])

    def view(at):
        ref, slot = at
        if slot is None:
            return refs[ref]
        if isinstance(slot, tuple):
            slot = lax.rem(here + 4 - slot[0], 4)
        return refs[ref].at[slot]

    def copies(i, g):
        ops = view(groups[i])
        parts = (
            (view(renewed[i]) if renewed else ops.at[0:STACK], left_buf.at[g]),
            (ops.at[STACK : 2 * STACK], right_buf.at[g]),
            (ops.at[2 * STACK : ROWS], mix_buf.at[g]),
        )
        return [pltpu.make_async_copy(a, b, sems.at[g, k]) for k, (a, b) in enumerate(parts)]

    for i in range(len(groups)):
        for copy in copies(i, i):
            copy.start()
    total[...] = start[...] if starts else jnp.zeros_like(total)

    def body(g, carry):
        for copy in copies(0, g):
            copy.wait()
        left = left_buf[g]
        lifted = [
            jnp.dot(left, field[s * BLOCK : (s + 1) * BLOCK], preferred_element_type=F32)
            for s in range(LOCAL)
        ]
        parts = mix_buf[g].astype(F32)
        mix = parts[0:1] + parts[1:2] + parts[2:3]
        columns = [[] for _ in range(LOCAL)]
        for t in range(TERMS):
            rows = slice(t * BLOCK, (t + 1) * BLOCK)
            for s in range(LOCAL):
                mixed = None
                for s2 in range(LOCAL):
                    at = t * 16 + s * LOCAL + s2
                    term = mix[:, at : at + 1] * lifted[s2][rows]
                    mixed = term if mixed is None else mixed + term
                columns[s].append(mixed.astype(BF16))
        right = jnp.concatenate(
            [right_buf[g, t * BLOCK : (t + 1) * BLOCK] for t in range(TERMS)], axis=1
        )
        for s in range(LOCAL):
            total[s * BLOCK : (s + 1) * BLOCK] += lax.dot_general(
                jnp.concatenate(columns[s], axis=1),
                right,
                (((1,), (1,)), ((), ())),
                preferred_element_type=F32,
            )
        return carry

    lax.fori_loop(0, len(groups), body, 0)
    out[...] = total[...].astype(out.dtype)


def listed(arrays, base, distances):
    out = []
    for n, value in enumerate(arrays):
        slots = [None]
        if value.ndim == 3:
            slots = [(1,), (2,), (3,), (0,)] if distances else [0, 1, 2, 3]
        out += [(base + n, slot) for slot in slots]
    return out


def apply_terms(place, field, ops, renewed=(), start=None, kind=BF16):
    at_ops = listed(ops, 0, bool(renewed))
    groups = len(at_ops)
    at_renewed = listed(renewed, len(ops), False)
    starts = start is not None
    name = "apply_moved" if renewed else "apply_terms"
    return pl.pallas_call(
        functools.partial(apply_kernel, at_ops, at_renewed, starts),
        in_specs=[SMEM, VMEM] + [ANY] * (len(ops) + len(renewed)) + [VMEM] * starts,
        out_specs=VMEM,
        out_shape=jax.ShapeDtypeStruct((LOCAL * BLOCK, BLOCK), kind),
        scratch_shapes=[
            pltpu.VMEM((groups, STACK, BLOCK), BF16),
            pltpu.VMEM((groups, STACK, BLOCK), BF16),
            pltpu.VMEM((groups, MIX_ROWS, BLOCK), BF16),
            pltpu.VMEM((LOCAL * BLOCK, BLOCK), F32),
            pltpu.SemaphoreType.DMA((groups, 3)),
        ],
        compiler_params=pltpu.CompilerParams(vmem_limit_bytes=60 << 20),
        name=f"{name}_{groups}_{int(starts)}",
        cost_estimate=pl.CostEstimate(flops=1 << 20, bytes_accessed=1 << 16, transcendentals=0),
    )(place, field, *ops, *renewed, *([start] if starts else []))


def reduce_chunks(partial):
    parts = exchange(partial.reshape(8, CHUNK, BLOCK), HOLDERS)
    return jnp.sum(parts.astype(F32), axis=0).astype(BF16)


def after(value, *others):
    return lax.optimization_barrier((value, *others))[0]


def spread(rows):
    whole = exchange(jnp.broadcast_to(rows[None], (8, CHUNK, BLOCK)), HOLDERS)
    return whole.reshape(LOCAL * BLOCK, BLOCK)


def shards(wave, left_ops, right_ops, site_ops, reach, pairing, site_tensor):
    pair = pairing[0]
    me = lax.axis_index("op")
    place = jnp.stack([me >> 4, (me >> 1) & 3, me & 1]).astype(jnp.int32)

    own_rows = lax.ppermute(wave[0], "op", TO_HOLDERS)
    kept, *passed = pack(place, pair, site_ops.reshape(-1), reach[0], left_ops, right_ops)
    field = spread(own_rows)
    kept, *passed = lax.optimization_barrier((kept, *passed, field))[:5]
    packed = after(place, kept)
    kept = exchange(kept, LINES)
    passed = [lax.ppermute(passed[d], "op", along(d, 1)) for d in (1, 2, 3, 0)]
    renewed_passed = renew(False, packed, pair, left_ops, site_tensor)
    renewed_kept = renew(True, after(place, renewed_passed), pair, left_ops, site_tensor)
    renewed = []
    for value, flip in ((renewed_kept, 0), (renewed_passed, 1)):
        hop = lax.ppermute(value, "sect", [(0, 1), (1, 0)]).reshape(4, STACK, BLOCK)
        renewed += [
            lax.ppermute(hop[d], "op", along(d, flip)) if d + flip else hop[d] for d in (1, 2, 3, 0)
        ]

    partial = apply_terms(place, field, [kept, *passed])
    first = reduce_chunks(partial)
    first_own = lax.ppermute(first, "op", TO_OWNERS)
    first_field = spread(first)
    first_field, *renewed = lax.optimization_barrier((first_field, *renewed))
    partial = apply_terms(place, first_field, [kept, *passed])
    second = reduce_chunks(partial)
    second_own = lax.ppermute(second, "op", TO_OWNERS)

    partial = apply_terms(place, after(field, partial), [kept, *passed], renewed)
    moved = reduce_chunks(after(partial, second))
    moved_own = lax.ppermute(moved, "op", TO_OWNERS)
    return first_own[None], second_own[None], moved_own[None]


def solution(mesh):
    placed = (
        P("sect", "op", None),
        P("sect", "op", None, None, None),
        P("sect", "op", None, None, None),
        P("sect", "op", None, None),
        P("sect", "op"),
        P("sect", None),
        P("sect", None, None, None, None),
    )
    return jax.shard_map(
        shards,
        mesh=mesh,
        in_specs=placed,
        out_specs=(P("sect", "op", None), P("sect", "op", None), P("sect", "op", None)),
        check_vma=False,
    )
```

```python
import functools

import jax
import jax.numpy as jnp
from jax import lax
from jax.experimental import pallas as pl
from jax.experimental.pallas import tpu as pltpu
from jax.sharding import PartitionSpec as P

NX, NY, NZ, NC = 4, 2, 4, 2
DEVICES = NX * NY * NZ * NC
SECTORS = 8
LOCAL = 4
BLOCK = 256
CHUNK = 128
TERMS = 3
STACK = TERMS * BLOCK
MIX_ROWS = 16
ROWS = 2 * STACK + MIX_ROWS
BF16 = jnp.bfloat16
F32 = jnp.float32
ANY = pl.BlockSpec(memory_space=pl.ANY)
SMEM = pl.BlockSpec(memory_space=pltpu.SMEM)
VMEM = pl.BlockSpec(memory_space=pltpu.VMEM)


def device_at(x, y, z, c):
    return (((x % NX) * NY + y) * NZ + z % NZ) * NC + c


PLACES = [
    (x, y, z, c) for x in range(NX) for y in range(NY) for z in range(NZ) for c in range(NC)
]
HOLDERS = [
    [device_at(x, y, half - x, c) for x in range(NX) for y in range(NY)]
    for half in range(SECTORS // NC)
    for c in range(NC)
]
OWNERS = [[q * 8 + k for k in range(8)] for q in range(SECTORS)]
TO_HOLDERS = [(OWNERS[q][k], HOLDERS[q][k]) for q in range(SECTORS) for k in range(8)]
TO_OWNERS = [(HOLDERS[q][k], OWNERS[q][k]) for q in range(SECTORS) for k in range(8)]
LINES = [[device_at(x, y, z, 0) for x in range(NX)] for y in range(NY) for z in range(NZ)]
LINES += [[device_at(x, y, z, 1) for z in range(NZ)] for x in range(NX) for y in range(NY)]


def along(d, flip):
    return [
        (
            device_at(x, y, z, c),
            device_at(x + d * (1 - c), y, z + d * c, c ^ flip),
        )
        for x, y, z, c in PLACES
    ]


def exchange(value, groups):
    return lax.all_to_all(value, "op", 0, 0, axis_index_groups=groups)


def mixer_rows(row, held, sector):
    value = jnp.where(sector < held, row, 0.0)
    high = value.astype(BF16).astype(F32)
    middle = (value - high).astype(BF16).astype(F32)
    low = value - high - middle
    at = lax.broadcasted_iota(jnp.int32, (MIX_ROWS, BLOCK), 0)
    parts = jnp.where(at == 0, high, jnp.where(at == 1, middle, jnp.where(at == 2, low, 0.0)))
    return parts.astype(BF16)


def pack_kernel(place, pair, site, reach, left, right, *refs):
    outs = refs[:5]
    left_buf, right_buf, mix_buf, load_sems, sems = refs[5:]
    x, z, c = place[0], place[1], place[2]
    loads = []
    for t in range(TERMS):
        loads.append(pltpu.make_async_copy(left.at[0, t], left_buf.at[t], load_sems.at[t, 0]))
        loads.append(pltpu.make_async_copy(right.at[0, t], right_buf.at[t], load_sems.at[t, 1]))
    for copy in loads:
        copy.start()
    lane = lax.broadcasted_iota(jnp.int32, (1, BLOCK), 1)
    row = jnp.zeros((1, BLOCK), F32)
    held = jnp.zeros((1, BLOCK), jnp.int32)
    for t in range(TERMS):
        held = jnp.where(lane // 16 == t, reach[t], held)
        for e in range(LOCAL * LOCAL):
            row = jnp.where(lane == t * 16 + e, site[t * 16 + e], row)
    sectors = [lax.rem(i + jnp.where(c == 0, z, x), 4) * 2 + c for i in range(4)]
    sectors += [lax.rem(x + z + d, 4) * 2 + 1 - c for d in range(4)]
    places = [outs[0].at[i] for i in range(4)] + list(outs[1:])
    stores = []

    def store(src, dst):
        stores.append(pltpu.make_async_copy(src, dst, sems.at[len(stores)]))
        stores[-1].start()

    for i, q in enumerate(sectors):
        mix_buf[i] = mixer_rows(row, held, q)
    for i in range(8):
        store(mix_buf.at[i], places[i].at[2 * STACK : ROWS])
    for copy in loads:
        copy.wait()
    for i, q in enumerate(sectors):
        for t in range(TERMS):
            store(left_buf.at[t, q], places[i].at[t * BLOCK : (t + 1) * BLOCK])
            store(right_buf.at[t, pair[q]], places[i].at[STACK + t * BLOCK : STACK + (t + 1) * BLOCK])
    for copy in stores:
        copy.wait()


def pack(place, pair, site, reach, left_ops, right_ops):
    return pl.pallas_call(
        pack_kernel,
        in_specs=[SMEM, SMEM, SMEM, SMEM, ANY, ANY],
        out_specs=[ANY] * 5,
        out_shape=[jax.ShapeDtypeStruct((4, ROWS, BLOCK), BF16)]
        + [jax.ShapeDtypeStruct((ROWS, BLOCK), BF16)] * 4,
        scratch_shapes=[
            pltpu.VMEM((TERMS, SECTORS, BLOCK, BLOCK), BF16),
            pltpu.VMEM((TERMS, SECTORS, BLOCK, BLOCK), BF16),
            pltpu.VMEM((8, MIX_ROWS, BLOCK), BF16),
            pltpu.SemaphoreType.DMA((TERMS, 2)),
            pltpu.SemaphoreType.DMA((56,)),
        ],
        compiler_params=pltpu.CompilerParams(vmem_limit_bytes=56 << 20),
        name="pack",
        cost_estimate=pl.CostEstimate(flops=1 << 20, bytes_accessed=1 << 16, transcendentals=0),
    )(place, pair, site, reach, left_ops, right_ops)


def renew_kernel(place, pair, left, tensor, out):
    lefts = left[0, :, 0].reshape(STACK, BLOCK)
    lifted = []
    sites = []
    for s in range(LOCAL):
        site = tensor[0, 0, s]
        lifted.append(jnp.dot(lefts, site, preferred_element_type=F32).astype(BF16))
        sites.append(site.T)
    sites = jnp.concatenate(sites, axis=1)
    for t in range(TERMS):
        stacked = jnp.concatenate([lifted[s][t * BLOCK : (t + 1) * BLOCK] for s in range(LOCAL)])
        out[0, t] = jnp.dot(sites, stacked, preferred_element_type=F32).astype(BF16)


def renew(kept, place, pair, left_ops, tensor):
    def left_sector(i, place, pair):
        x, z, c = place[0], place[1], place[2]
        wanted = lax.rem(x + z + i, 4) * 2 + (c if kept else 1 - c)
        q = jnp.int32(0)
        for k in range(1, SECTORS):
            q = jnp.where(pair[k] == wanted, k, q)
        return q

    grid_spec = pltpu.PrefetchScalarGridSpec(
        num_scalar_prefetch=2,
        grid=(4,),
        in_specs=[
            pl.BlockSpec((1, TERMS, 1, BLOCK, BLOCK), lambda d, *s: (0, 0, left_sector(d, *s), 0, 0)),
            pl.BlockSpec((1, 1, LOCAL, BLOCK, BLOCK), lambda d, *s: (0, left_sector(d, *s), 0, 0, 0)),
        ],
        out_specs=pl.BlockSpec((1, TERMS, BLOCK, BLOCK), lambda d, *s: (d, 0, 0, 0)),
    )
    return pl.pallas_call(
        renew_kernel,
        grid_spec=grid_spec,
        out_shape=jax.ShapeDtypeStruct((4, TERMS, BLOCK, BLOCK), BF16),
        name="renew_kept" if kept else "renew_swapped",
        cost_estimate=pl.CostEstimate(
            flops=12 * 8 * 2 * BLOCK**3, bytes_accessed=20 << 20, transcendentals=0
        ),
    )(place, pair, left_ops, tensor)


def apply_kernel(groups, renewed, starts, place, field, *refs):
    out, left_buf, right_buf, mix_buf, total, sems = refs[-6:]
    start = refs[-7] if starts else None

    here = jnp.where(place[2] == 0, place[0], place[1])

    def view(at):
        ref, slot = at
        if slot is None:
            return refs[ref]
        if isinstance(slot, tuple):
            slot = lax.rem(here + 4 - slot[0], 4)
        return refs[ref].at[slot]

    def copies(i, g):
        ops = view(groups[i])
        parts = (
            (view(renewed[i]) if renewed else ops.at[0:STACK], left_buf.at[g]),
            (ops.at[STACK : 2 * STACK], right_buf.at[g]),
            (ops.at[2 * STACK : ROWS], mix_buf.at[g]),
        )
        return [pltpu.make_async_copy(a, b, sems.at[g, k]) for k, (a, b) in enumerate(parts)]

    for i in range(len(groups)):
        for copy in copies(i, i):
            copy.start()
    total[...] = start[...] if starts else jnp.zeros_like(total)

    def body(g, carry):
        for copy in copies(0, g):
            copy.wait()
        left = left_buf[g]
        lifted = [
            jnp.dot(left, field[s * BLOCK : (s + 1) * BLOCK], preferred_element_type=F32)
            for s in range(LOCAL)
        ]
        parts = mix_buf[g].astype(F32)
        mix = parts[0:1] + parts[1:2] + parts[2:3]
        columns = [[] for _ in range(LOCAL)]
        for t in range(TERMS):
            rows = slice(t * BLOCK, (t + 1) * BLOCK)
            for s in range(LOCAL):
                mixed = None
                for s2 in range(LOCAL):
                    at = t * 16 + s * LOCAL + s2
                    term = mix[:, at : at + 1] * lifted[s2][rows]
                    mixed = term if mixed is None else mixed + term
                columns[s].append(mixed.astype(BF16))
        right = jnp.concatenate(
            [right_buf[g, t * BLOCK : (t + 1) * BLOCK] for t in range(TERMS)], axis=1
        )
        for s in range(LOCAL):
            total[s * BLOCK : (s + 1) * BLOCK] += lax.dot_general(
                jnp.concatenate(columns[s], axis=1),
                right,
                (((1,), (1,)), ((), ())),
                preferred_element_type=F32,
            )
        return carry

    lax.fori_loop(0, len(groups), body, 0)
    out[...] = total[...].astype(out.dtype)


def listed(arrays, base, distances):
    out = []
    for n, value in enumerate(arrays):
        slots = [None]
        if value.ndim == 3:
            slots = [(1,), (2,), (3,), (0,)] if distances else [0, 1, 2, 3]
        out += [(base + n, slot) for slot in slots]
    return out


def apply_terms(place, field, ops, renewed=(), start=None, kind=BF16):
    at_ops = listed(ops, 0, bool(renewed))
    groups = len(at_ops)
    at_renewed = listed(renewed, len(ops), False)
    starts = start is not None
    name = "apply_moved" if renewed else "apply_terms"
    return pl.pallas_call(
        functools.partial(apply_kernel, at_ops, at_renewed, starts),
        in_specs=[SMEM, VMEM] + [ANY] * (len(ops) + len(renewed)) + [VMEM] * starts,
        out_specs=VMEM,
        out_shape=jax.ShapeDtypeStruct((LOCAL * BLOCK, BLOCK), kind),
        scratch_shapes=[
            pltpu.VMEM((groups, STACK, BLOCK), BF16),
            pltpu.VMEM((groups, STACK, BLOCK), BF16),
            pltpu.VMEM((groups, MIX_ROWS, BLOCK), BF16),
            pltpu.VMEM((LOCAL * BLOCK, BLOCK), F32),
            pltpu.SemaphoreType.DMA((groups, 3)),
        ],
        compiler_params=pltpu.CompilerParams(vmem_limit_bytes=60 << 20),
        name=f"{name}_{groups}_{int(starts)}",
        cost_estimate=pl.CostEstimate(
            flops=3 * groups * 8 * 2 * BLOCK**3, bytes_accessed=48 << 20, transcendentals=0
        ),
    )(place, field, *ops, *renewed, *([start] if starts else []))


def reduce_chunks(partial):
    parts = exchange(partial.reshape(8, CHUNK, BLOCK), HOLDERS)
    return jnp.sum(parts.astype(F32), axis=0).astype(BF16)


def after(value, *others):
    return lax.optimization_barrier((value, *others))[0]


def spread(rows):
    whole = exchange(jnp.broadcast_to(rows[None], (8, CHUNK, BLOCK)), HOLDERS)
    return whole.reshape(LOCAL * BLOCK, BLOCK)


def shards(wave, left_ops, right_ops, site_ops, reach, pairing, site_tensor):
    pair = pairing[0]
    me = lax.axis_index("op")
    place = jnp.stack([me >> 4, (me >> 1) & 3, me & 1]).astype(jnp.int32)

    own_rows = lax.ppermute(wave[0], "op", TO_HOLDERS)
    renewed_kept = renew(True, place, pair, left_ops, site_tensor)
    field = spread(after(own_rows, renewed_kept))
    kept, *passed = pack(
        after(place, renewed_kept, own_rows),
        pair,
        site_ops.reshape(-1),
        reach[0],
        left_ops,
        right_ops,
    )
    kept, *passed, renewed_kept, later, field = lax.optimization_barrier(
        (kept, *passed, renewed_kept, place, field)
    )
    kept = exchange(kept, LINES)
    passed = [lax.ppermute(passed[d], "op", along(d, 1)) for d in (1, 2, 3, 0)]
    renewed_passed = renew(False, later, pair, left_ops, site_tensor)
    near, far = [
        lax.ppermute(value, "sect", [(0, 1), (1, 0)]).reshape(4, STACK, BLOCK)
        for value in (renewed_kept, renewed_passed)
    ]
    near = [lax.ppermute(near[d], "op", along(d, 0)) for d in (1, 2, 3)] + [near[0]]
    far = [lax.ppermute(far[d], "op", along(d, 1)) for d in (1, 2, 3, 0)]

    partial = apply_terms(place, field, [kept, *passed])
    first = reduce_chunks(after(partial, *near))
    first_own = lax.ppermute(first, "op", TO_OWNERS)
    first_field, first_own = lax.optimization_barrier((spread(first), first_own))
    partial = apply_terms(place, first_field, [kept, *passed])
    second = reduce_chunks(partial)

    partial = apply_terms(place, after(field, partial), [kept, *passed], near + far)
    moved = reduce_chunks(after(partial, second))
    last = lax.ppermute(jnp.stack([second, moved]), "op", TO_OWNERS)
    return first_own[None], last[0:1], last[1:2]


def solution(mesh):
    placed = (
        P("sect", "op", None),
        P("sect", "op", None, None, None),
        P("sect", "op", None, None, None),
        P("sect", "op", None, None),
        P("sect", "op"),
        P("sect", None),
        P("sect", None, None, None, None),
    )
    return jax.shard_map(
        shards,
        mesh=mesh,
        in_specs=placed,
        out_specs=(P("sect", "op", None), P("sect", "op", None), P("sect", "op", None)),
        check_vma=False,
    )
```

```python
import functools

import jax
import jax.numpy as jnp
from jax import lax
from jax.experimental import pallas as pl
from jax.experimental.pallas import tpu as pltpu
from jax.sharding import PartitionSpec as P

NX, NY, NZ, NC = 4, 2, 4, 2
DEVICES = NX * NY * NZ * NC
SECTORS = 8
LOCAL = 4
BLOCK = 256
CHUNK = 128
TERMS = 3
STACK = TERMS * BLOCK
MIX_ROWS = 16
ROWS = 2 * STACK + MIX_ROWS
BF16 = jnp.bfloat16
F32 = jnp.float32
ANY = pl.BlockSpec(memory_space=pl.ANY)
SMEM = pl.BlockSpec(memory_space=pltpu.SMEM)
VMEM = pl.BlockSpec(memory_space=pltpu.VMEM)


def device_at(x, y, z, c):
    return (((x % NX) * NY + y) * NZ + z % NZ) * NC + c


PLACES = [
    (x, y, z, c) for x in range(NX) for y in range(NY) for z in range(NZ) for c in range(NC)
]
HOLDERS = [
    [device_at(x, y, half - x, c) for x in range(NX) for y in range(NY)]
    for half in range(SECTORS // NC)
    for c in range(NC)
]
OWNERS = [[q * 8 + k for k in range(8)] for q in range(SECTORS)]
TO_HOLDERS = [(OWNERS[q][k], HOLDERS[q][k]) for q in range(SECTORS) for k in range(8)]
TO_OWNERS = [(HOLDERS[q][k], OWNERS[q][k]) for q in range(SECTORS) for k in range(8)]
LINES = [[device_at(x, y, z, 0) for x in range(NX)] for y in range(NY) for z in range(NZ)]
LINES += [[device_at(x, y, z, 1) for z in range(NZ)] for x in range(NX) for y in range(NY)]


def along(d, flip):
    return [
        (
            device_at(x, y, z, c),
            device_at(x + d * (1 - c), y, z + d * c, c ^ flip),
        )
        for x, y, z, c in PLACES
    ]


def exchange(value, groups):
    return lax.all_to_all(value, "op", 0, 0, axis_index_groups=groups)


def mixer_rows(row, held, sector):
    value = jnp.where(sector < held, row, 0.0)
    high = value.astype(BF16).astype(F32)
    middle = (value - high).astype(BF16).astype(F32)
    low = value - high - middle
    at = lax.broadcasted_iota(jnp.int32, (MIX_ROWS, BLOCK), 0)
    parts = jnp.where(at == 0, high, jnp.where(at == 1, middle, jnp.where(at == 2, low, 0.0)))
    return parts.astype(BF16)


def pack_kernel(place, pair, site, reach, left, right, *refs):
    outs = refs[:5]
    left_buf, right_buf, mix_buf, load_sems, sems = refs[5:]
    x, z, c = place[0], place[1], place[2]
    loads = []
    for t in range(TERMS):
        loads.append(pltpu.make_async_copy(left.at[0, t], left_buf.at[t], load_sems.at[t, 0]))
        loads.append(pltpu.make_async_copy(right.at[0, t], right_buf.at[t], load_sems.at[t, 1]))
    for copy in loads:
        copy.start()
    lane = lax.broadcasted_iota(jnp.int32, (1, BLOCK), 1)
    row = jnp.zeros((1, BLOCK), F32)
    held = jnp.zeros((1, BLOCK), jnp.int32)
    for t in range(TERMS):
        held = jnp.where(lane // 16 == t, reach[t], held)
        for e in range(LOCAL * LOCAL):
            row = jnp.where(lane == t * 16 + e, site[t * 16 + e], row)
    sectors = [lax.rem(i + jnp.where(c == 0, z, x), 4) * 2 + c for i in range(4)]
    sectors += [lax.rem(x + z + d, 4) * 2 + 1 - c for d in range(4)]
    places = [outs[0].at[i] for i in range(4)] + list(outs[1:])
    stores = []

    def store(src, dst):
        stores.append(pltpu.make_async_copy(src, dst, sems.at[len(stores)]))
        stores[-1].start()

    for i, q in enumerate(sectors):
        mix_buf[i] = mixer_rows(row, held, q)
    for i in range(8):
        store(mix_buf.at[i], places[i].at[2 * STACK : ROWS])
    for copy in loads:
        copy.wait()
    for i, q in enumerate(sectors):
        for t in range(TERMS):
            store(left_buf.at[t, q], places[i].at[t * BLOCK : (t + 1) * BLOCK])
            store(right_buf.at[t, pair[q]], places[i].at[STACK + t * BLOCK : STACK + (t + 1) * BLOCK])
    for copy in stores:
        copy.wait()


def pack(place, pair, site, reach, left_ops, right_ops):
    return pl.pallas_call(
        pack_kernel,
        in_specs=[SMEM, SMEM, SMEM, SMEM, ANY, ANY],
        out_specs=[ANY] * 5,
        out_shape=[jax.ShapeDtypeStruct((4, ROWS, BLOCK), BF16)]
        + [jax.ShapeDtypeStruct((ROWS, BLOCK), BF16)] * 4,
        scratch_shapes=[
            pltpu.VMEM((TERMS, SECTORS, BLOCK, BLOCK), BF16),
            pltpu.VMEM((TERMS, SECTORS, BLOCK, BLOCK), BF16),
            pltpu.VMEM((8, MIX_ROWS, BLOCK), BF16),
            pltpu.SemaphoreType.DMA((TERMS, 2)),
            pltpu.SemaphoreType.DMA((56,)),
        ],
        compiler_params=pltpu.CompilerParams(vmem_limit_bytes=56 << 20),
        name="pack",
        cost_estimate=pl.CostEstimate(flops=1 << 20, bytes_accessed=1 << 16, transcendentals=0),
    )(place, pair, site, reach, left_ops, right_ops)


def renew_kernel(place, pair, left, tensor, out):
    lefts = left[0, :, 0].reshape(STACK, BLOCK)
    lifted = []
    sites = []
    for s in range(LOCAL):
        site = tensor[0, 0, s]
        lifted.append(jnp.dot(lefts, site, preferred_element_type=F32).astype(BF16))
        sites.append(site.T)
    sites = jnp.concatenate(sites, axis=1)
    for t in range(TERMS):
        stacked = jnp.concatenate([lifted[s][t * BLOCK : (t + 1) * BLOCK] for s in range(LOCAL)])
        out[0, t] = jnp.dot(sites, stacked, preferred_element_type=F32).astype(BF16)


def renew(kept, place, pair, left_ops, tensor):
    def left_sector(i, place, pair):
        x, z, c = place[0], place[1], place[2]
        wanted = lax.rem(x + z + i, 4) * 2 + (c if kept else 1 - c)
        q = jnp.int32(0)
        for k in range(1, SECTORS):
            q = jnp.where(pair[k] == wanted, k, q)
        return q

    grid_spec = pltpu.PrefetchScalarGridSpec(
        num_scalar_prefetch=2,
        grid=(4,),
        in_specs=[
            pl.BlockSpec((1, TERMS, 1, BLOCK, BLOCK), lambda d, *s: (0, 0, left_sector(d, *s), 0, 0)),
            pl.BlockSpec((1, 1, LOCAL, BLOCK, BLOCK), lambda d, *s: (0, left_sector(d, *s), 0, 0, 0)),
        ],
        out_specs=pl.BlockSpec((1, TERMS, BLOCK, BLOCK), lambda d, *s: (d, 0, 0, 0)),
    )
    return pl.pallas_call(
        renew_kernel,
        grid_spec=grid_spec,
        out_shape=jax.ShapeDtypeStruct((4, TERMS, BLOCK, BLOCK), BF16),
        name="renew_kept" if kept else "renew_swapped",
        cost_estimate=pl.CostEstimate(
            flops=12 * 8 * 2 * BLOCK**3, bytes_accessed=20 << 20, transcendentals=0
        ),
    )(place, pair, left_ops, tensor)


def apply_kernel(groups, renewed, starts, joins, place, field, *refs):
    out, left_buf, right_buf, mix_buf, total, sems = refs[-6:]

    here = jnp.where(place[2] == 0, place[0], place[1])

    def view(at):
        ref, slot = at
        if slot is None:
            return refs[ref]
        if isinstance(slot, tuple):
            slot = lax.rem(here + 4 - slot[0], 4)
        return refs[ref].at[slot]

    def copies(i, g):
        ops = view(groups[i])
        parts = (
            (view(renewed[i]) if renewed else ops.at[0:STACK], left_buf.at[g]),
            (ops.at[STACK : 2 * STACK], right_buf.at[g]),
            (ops.at[2 * STACK : ROWS], mix_buf.at[g]),
        )
        return [pltpu.make_async_copy(a, b, sems.at[g, k]) for k, (a, b) in enumerate(parts)]

    for i in range(len(groups)):
        for copy in copies(i, i):
            copy.start()
    total[...] = refs[-7 - joins][...] if starts else jnp.zeros_like(total)

    def body(g, carry):
        for copy in copies(0, g):
            copy.wait()
        left = left_buf[g]
        lifted = [
            jnp.dot(left, field[s * BLOCK : (s + 1) * BLOCK], preferred_element_type=F32)
            for s in range(LOCAL)
        ]
        parts = mix_buf[g].astype(F32)
        mix = parts[0:1] + parts[1:2] + parts[2:3]
        columns = [[] for _ in range(LOCAL)]
        for t in range(TERMS):
            rows = slice(t * BLOCK, (t + 1) * BLOCK)
            for s in range(LOCAL):
                mixed = None
                for s2 in range(LOCAL):
                    at = t * 16 + s * LOCAL + s2
                    term = mix[:, at : at + 1] * lifted[s2][rows]
                    mixed = term if mixed is None else mixed + term
                columns[s].append(mixed.astype(BF16))
        right = jnp.concatenate(
            [right_buf[g, t * BLOCK : (t + 1) * BLOCK] for t in range(TERMS)], axis=1
        )
        for s in range(LOCAL):
            total[s * BLOCK : (s + 1) * BLOCK] += lax.dot_general(
                jnp.concatenate(columns[s], axis=1),
                right,
                (((1,), (1,)), ((), ())),
                preferred_element_type=F32,
            )
        return carry

    lax.fori_loop(0, len(groups), body, 0)
    if joins:
        other = refs[-7]
        for k in range(8):
            rows = slice(k * CHUNK, (k + 1) * CHUNK)
            out[k, 0] = other[rows]
            out[k, 1] = total[rows].astype(BF16)
    else:
        out[...] = total[...].astype(out.dtype)


def listed(arrays, base, distances):
    out = []
    for n, value in enumerate(arrays):
        slots = [None]
        if value.ndim == 3:
            slots = [(1,), (2,), (3,), (0,)] if distances else [0, 1, 2, 3]
        out += [(base + n, slot) for slot in slots]
    return out


def apply_terms(place, field, ops, renewed=(), start=None, other=None, kind=BF16):
    at_ops = listed(ops, 0, bool(renewed))
    groups = len(at_ops)
    at_renewed = listed(renewed, len(ops), False)
    starts, joins = start is not None, other is not None
    extra = [value for value in (start, other) if value is not None]
    shape = (8, 2, CHUNK, BLOCK) if joins else (LOCAL * BLOCK, BLOCK)
    name = "apply_moved" if renewed else "apply_terms"
    return pl.pallas_call(
        functools.partial(apply_kernel, at_ops, at_renewed, starts, joins),
        in_specs=[SMEM, VMEM] + [ANY] * (len(ops) + len(renewed)) + [VMEM] * len(extra),
        out_specs=VMEM,
        out_shape=jax.ShapeDtypeStruct(shape, kind),
        scratch_shapes=[
            pltpu.VMEM((groups, STACK, BLOCK), BF16),
            pltpu.VMEM((groups, STACK, BLOCK), BF16),
            pltpu.VMEM((groups, MIX_ROWS, BLOCK), BF16),
            pltpu.VMEM((LOCAL * BLOCK, BLOCK), F32),
            pltpu.SemaphoreType.DMA((groups, 3)),
        ],
        compiler_params=pltpu.CompilerParams(vmem_limit_bytes=60 << 20),
        name=f"{name}_{groups}",
        cost_estimate=pl.CostEstimate(
            flops=3 * groups * 8 * 2 * BLOCK**3, bytes_accessed=48 << 20, transcendentals=0
        ),
    )(place, field, *ops, *renewed, *extra)


def reduce_chunks(partial):
    parts = exchange(partial, HOLDERS)
    return jnp.sum(parts.astype(F32), axis=0).astype(BF16)


def after(value, *others):
    return lax.optimization_barrier((value, *others))[0]


def spread(rows):
    whole = exchange(jnp.broadcast_to(rows[None], (8, CHUNK, BLOCK)), HOLDERS)
    return whole.reshape(LOCAL * BLOCK, BLOCK)


def shards(wave, left_ops, right_ops, site_ops, reach, pairing, site_tensor):
    pair = pairing[0]
    me = lax.axis_index("op")
    place = jnp.stack([me >> 4, (me >> 1) & 3, me & 1]).astype(jnp.int32)

    own_rows = lax.ppermute(wave[0], "op", TO_HOLDERS)
    renewed_kept = renew(True, place, pair, left_ops, site_tensor)
    field = spread(after(own_rows, renewed_kept))
    kept, *passed = pack(
        after(place, renewed_kept, own_rows),
        pair,
        site_ops.reshape(-1),
        reach[0],
        left_ops,
        right_ops,
    )
    kept, *passed, renewed_kept, later, field = lax.optimization_barrier(
        (kept, *passed, renewed_kept, place, field)
    )
    kept = exchange(kept, LINES)
    passed = [lax.ppermute(passed[d], "op", along(d, 1)) for d in (1, 2, 3, 0)]
    renewed_passed = renew(False, later, pair, left_ops, site_tensor)
    near, far = [
        lax.ppermute(value, "sect", [(0, 1), (1, 0)]).reshape(4, STACK, BLOCK)
        for value in (renewed_kept, renewed_passed)
    ]
    near = [lax.ppermute(near[d], "op", along(d, 0)) for d in (1, 2, 3)] + [near[0]]
    far = [lax.ppermute(far[d], "op", along(d, 1)) for d in (1, 2, 3, 0)]

    partial = apply_terms(place, field, [kept, *passed])
    half = apply_terms(place, field, [kept], near, kind=F32)
    first = reduce_chunks(after(partial, *near).reshape(8, 1, CHUNK, BLOCK))
    first, half = lax.optimization_barrier((first, half))
    first_field = spread(first[0])
    partial = apply_terms(place, first_field, [kept, *passed])
    partial = apply_terms(place, after(field, partial), passed, far, half, partial)
    images = jnp.concatenate([first, reduce_chunks(partial)])
    images = lax.ppermute(images, "op", TO_OWNERS)
    return images[0:1], images[1:2], images[2:3]


def solution(mesh):
    placed = (
        P("sect", "op", None),
        P("sect", "op", None, None, None),
        P("sect", "op", None, None, None),
        P("sect", "op", None, None),
        P("sect", "op"),
        P("sect", None),
        P("sect", None, None, None, None),
    )
    return jax.shard_map(
        shards,
        mesh=mesh,
        in_specs=placed,
        out_specs=(P("sect", "op", None), P("sect", "op", None), P("sect", "op", None)),
        check_vma=False,
    )
```

```python
import functools

import jax
import jax.numpy as jnp
from jax import lax
from jax.experimental import pallas as pl
from jax.experimental.pallas import tpu as pltpu
from jax.sharding import PartitionSpec as P

NX, NY, NZ, NC = 4, 2, 4, 2
DEVICES = NX * NY * NZ * NC
SECTORS = 8
LOCAL = 4
BLOCK = 256
CHUNK = 128
TERMS = 3
STACK = TERMS * BLOCK
MIX_ROWS = 16
ROWS = 2 * STACK + MIX_ROWS
BF16 = jnp.bfloat16
F32 = jnp.float32
ANY = pl.BlockSpec(memory_space=pl.ANY)
SMEM = pl.BlockSpec(memory_space=pltpu.SMEM)
VMEM = pl.BlockSpec(memory_space=pltpu.VMEM)


def device_at(x, y, z, c):
    return (((x % NX) * NY + y) * NZ + z % NZ) * NC + c


PLACES = [
    (x, y, z, c) for x in range(NX) for y in range(NY) for z in range(NZ) for c in range(NC)
]
HOLDERS = [
    [device_at(x, y, half - x, c) for x in range(NX) for y in range(NY)]
    for half in range(SECTORS // NC)
    for c in range(NC)
]
OWNERS = [[q * 8 + k for k in range(8)] for q in range(SECTORS)]
TO_HOLDERS = [(OWNERS[q][k], HOLDERS[q][k]) for q in range(SECTORS) for k in range(8)]
TO_OWNERS = [(HOLDERS[q][k], OWNERS[q][k]) for q in range(SECTORS) for k in range(8)]
LINES = [[device_at(x, y, z, 0) for x in range(NX)] for y in range(NY) for z in range(NZ)]
LINES += [[device_at(x, y, z, 1) for z in range(NZ)] for x in range(NX) for y in range(NY)]


def along(d, flip):
    return [
        (
            device_at(x, y, z, c),
            device_at(x + d * (1 - c), y, z + d * c, c ^ flip),
        )
        for x, y, z, c in PLACES
    ]


def exchange(value, groups):
    return lax.all_to_all(value, "op", 0, 0, axis_index_groups=groups)


def mixer_rows(row, held, sector):
    value = jnp.where(sector < held, row, 0.0)
    high = value.astype(BF16).astype(F32)
    middle = (value - high).astype(BF16).astype(F32)
    low = value - high - middle
    at = lax.broadcasted_iota(jnp.int32, (MIX_ROWS, BLOCK), 0)
    parts = jnp.where(at == 0, high, jnp.where(at == 1, middle, jnp.where(at == 2, low, 0.0)))
    return parts.astype(BF16)


def pack_kernel(place, pair, site, reach, left, right, *refs):
    outs = refs[:5]
    left_buf, right_buf, mix_buf, load_sems, sems = refs[5:]
    x, z, c = place[0], place[1], place[2]
    loads = []
    for t in range(TERMS):
        loads.append(pltpu.make_async_copy(left.at[0, t], left_buf.at[t], load_sems.at[t, 0]))
        loads.append(pltpu.make_async_copy(right.at[0, t], right_buf.at[t], load_sems.at[t, 1]))
    for copy in loads:
        copy.start()
    lane = lax.broadcasted_iota(jnp.int32, (1, BLOCK), 1)
    row = jnp.zeros((1, BLOCK), F32)
    held = jnp.zeros((1, BLOCK), jnp.int32)
    for t in range(TERMS):
        held = jnp.where(lane // 16 == t, reach[t], held)
        for e in range(LOCAL * LOCAL):
            row = jnp.where(lane == t * 16 + e, site[t * 16 + e], row)
    sectors = [lax.rem(i + jnp.where(c == 0, z, x), 4) * 2 + c for i in range(4)]
    sectors += [lax.rem(x + z + d, 4) * 2 + 1 - c for d in range(4)]
    places = [outs[0].at[i] for i in range(4)] + list(outs[1:])
    stores = []

    def store(src, dst):
        stores.append(pltpu.make_async_copy(src, dst, sems.at[len(stores)]))
        stores[-1].start()

    for i, q in enumerate(sectors):
        mix_buf[i] = mixer_rows(row, held, q)
    for i in range(8):
        store(mix_buf.at[i], places[i].at[2 * STACK : ROWS])
    for copy in loads:
        copy.wait()
    for i, q in enumerate(sectors):
        for t in range(TERMS):
            store(left_buf.at[t, q], places[i].at[t * BLOCK : (t + 1) * BLOCK])
            store(right_buf.at[t, pair[q]], places[i].at[STACK + t * BLOCK : STACK + (t + 1) * BLOCK])
    for copy in stores:
        copy.wait()


def pack(place, pair, site, reach, left_ops, right_ops):
    return pl.pallas_call(
        pack_kernel,
        in_specs=[SMEM, SMEM, SMEM, SMEM, ANY, ANY],
        out_specs=[ANY] * 5,
        out_shape=[jax.ShapeDtypeStruct((4, ROWS, BLOCK), BF16)]
        + [jax.ShapeDtypeStruct((ROWS, BLOCK), BF16)] * 4,
        scratch_shapes=[
            pltpu.VMEM((TERMS, SECTORS, BLOCK, BLOCK), BF16),
            pltpu.VMEM((TERMS, SECTORS, BLOCK, BLOCK), BF16),
            pltpu.VMEM((8, MIX_ROWS, BLOCK), BF16),
            pltpu.SemaphoreType.DMA((TERMS, 2)),
            pltpu.SemaphoreType.DMA((56,)),
        ],
        compiler_params=pltpu.CompilerParams(vmem_limit_bytes=56 << 20),
        name="pack",
        cost_estimate=pl.CostEstimate(flops=1 << 20, bytes_accessed=1 << 16, transcendentals=0),
    )(place, pair, site, reach, left_ops, right_ops)


def renew_kernel(place, pair, left, tensor, out):
    lefts = left[0, :, 0].reshape(STACK, BLOCK)
    lifted = []
    sites = []
    for s in range(LOCAL):
        site = tensor[0, 0, s]
        lifted.append(jnp.dot(lefts, site, preferred_element_type=F32).astype(BF16))
        sites.append(site.T)
    sites = jnp.concatenate(sites, axis=1)
    for t in range(TERMS):
        stacked = jnp.concatenate([lifted[s][t * BLOCK : (t + 1) * BLOCK] for s in range(LOCAL)])
        out[0, t] = jnp.dot(sites, stacked, preferred_element_type=F32).astype(BF16)


def renew(kept, place, pair, left_ops, tensor):
    def left_sector(i, place, pair):
        x, z, c = place[0], place[1], place[2]
        wanted = lax.rem(x + z + i, 4) * 2 + (c if kept else 1 - c)
        q = jnp.int32(0)
        for k in range(1, SECTORS):
            q = jnp.where(pair[k] == wanted, k, q)
        return q

    grid_spec = pltpu.PrefetchScalarGridSpec(
        num_scalar_prefetch=2,
        grid=(4,),
        in_specs=[
            pl.BlockSpec((1, TERMS, 1, BLOCK, BLOCK), lambda d, *s: (0, 0, left_sector(d, *s), 0, 0)),
            pl.BlockSpec((1, 1, LOCAL, BLOCK, BLOCK), lambda d, *s: (0, left_sector(d, *s), 0, 0, 0)),
        ],
        out_specs=pl.BlockSpec((1, TERMS, BLOCK, BLOCK), lambda d, *s: (d, 0, 0, 0)),
    )
    return pl.pallas_call(
        renew_kernel,
        grid_spec=grid_spec,
        out_shape=jax.ShapeDtypeStruct((4, TERMS, BLOCK, BLOCK), BF16),
        name="renew_kept" if kept else "renew_swapped",
        cost_estimate=pl.CostEstimate(
            flops=12 * 8 * 2 * BLOCK**3, bytes_accessed=20 << 20, transcendentals=0
        ),
    )(place, pair, left_ops, tensor)


def apply_kernel(groups, renewed, starts, joins, place, field, *refs):
    out, left_buf, right_buf, mix_buf, total, sems = refs[-6:]

    here = jnp.where(place[2] == 0, place[0], place[1])

    def view(at):
        ref, slot = at
        if slot is None:
            return refs[ref]
        if isinstance(slot, tuple):
            slot = lax.rem(here + 4 - slot[0], 4)
        return refs[ref].at[slot]

    def copies(i, g):
        ops = view(groups[i])
        parts = (
            (view(renewed[i]) if renewed else ops.at[0:STACK], left_buf.at[g]),
            (ops.at[STACK : 2 * STACK], right_buf.at[g]),
            (ops.at[2 * STACK : ROWS], mix_buf.at[g]),
        )
        return [pltpu.make_async_copy(a, b, sems.at[g, k]) for k, (a, b) in enumerate(parts)]

    for i in range(len(groups)):
        for copy in copies(i, i):
            copy.start()
    total[...] = refs[-7 - joins][...] if starts else jnp.zeros_like(total)

    def body(g, carry):
        for copy in copies(0, g):
            copy.wait()
        left = left_buf[g]
        lifted = [
            jnp.dot(left, field[s * BLOCK : (s + 1) * BLOCK], preferred_element_type=F32)
            for s in range(LOCAL)
        ]
        parts = mix_buf[g].astype(F32)
        mix = parts[0:1] + parts[1:2] + parts[2:3]
        columns = [[] for _ in range(LOCAL)]
        for t in range(TERMS):
            rows = slice(t * BLOCK, (t + 1) * BLOCK)
            for s in range(LOCAL):
                mixed = None
                for s2 in range(LOCAL):
                    at = t * 16 + s * LOCAL + s2
                    term = mix[:, at : at + 1] * lifted[s2][rows]
                    mixed = term if mixed is None else mixed + term
                columns[s].append(mixed.astype(BF16))
        right = jnp.concatenate(
            [right_buf[g, t * BLOCK : (t + 1) * BLOCK] for t in range(TERMS)], axis=1
        )
        for s in range(LOCAL):
            total[s * BLOCK : (s + 1) * BLOCK] += lax.dot_general(
                jnp.concatenate(columns[s], axis=1),
                right,
                (((1,), (1,)), ((), ())),
                preferred_element_type=F32,
            )
        return carry

    lax.fori_loop(0, len(groups), body, 0)
    if joins:
        other = refs[-7]
        for k in range(8):
            rows = slice(k * CHUNK, (k + 1) * CHUNK)
            out[k, 0] = other[rows]
            out[k, 1] = total[rows].astype(BF16)
    else:
        out[...] = total[...].astype(out.dtype)


def listed(arrays, base, distances):
    out = []
    for n, value in enumerate(arrays):
        slots = [None]
        if value.ndim == 3:
            slots = [(1,), (2,), (3,), (0,)] if distances else [0, 1, 2, 3]
        out += [(base + n, slot) for slot in slots]
    return out


def apply_terms(place, field, ops, renewed=(), start=None, other=None, kind=BF16):
    at_ops = listed(ops, 0, bool(renewed))
    groups = len(at_ops)
    at_renewed = listed(renewed, len(ops), False)
    starts, joins = start is not None, other is not None
    extra = [value for value in (start, other) if value is not None]
    shape = (8, 2, CHUNK, BLOCK) if joins else (LOCAL * BLOCK, BLOCK)
    name = "apply_moved" if renewed else "apply_terms"
    return pl.pallas_call(
        functools.partial(apply_kernel, at_ops, at_renewed, starts, joins),
        in_specs=[SMEM, VMEM] + [ANY] * (len(ops) + len(renewed)) + [VMEM] * len(extra),
        out_specs=VMEM,
        out_shape=jax.ShapeDtypeStruct(shape, kind),
        scratch_shapes=[
            pltpu.VMEM((groups, STACK, BLOCK), BF16),
            pltpu.VMEM((groups, STACK, BLOCK), BF16),
            pltpu.VMEM((groups, MIX_ROWS, BLOCK), BF16),
            pltpu.VMEM((LOCAL * BLOCK, BLOCK), F32),
            pltpu.SemaphoreType.DMA((groups, 3)),
        ],
        compiler_params=pltpu.CompilerParams(vmem_limit_bytes=60 << 20),
        name=f"{name}_{groups}",
        cost_estimate=pl.CostEstimate(
            flops=3 * groups * 8 * 2 * BLOCK**3, bytes_accessed=48 << 20, transcendentals=0
        ),
    )(place, field, *ops, *renewed, *extra)


def reduce_chunks(partial):
    parts = exchange(partial, HOLDERS)
    return jnp.sum(parts.astype(F32), axis=0).astype(BF16)


def sum_kernel(parts, total, copies):
    value = parts[0, 0].astype(F32)
    for k in range(1, 8):
        value += parts[k, 0].astype(F32)
    value = value.astype(BF16)
    total[0] = value
    for k in range(8):
        copies[k] = value


def sum_and_copy(parts):
    return pl.pallas_call(
        sum_kernel,
        in_specs=[VMEM],
        out_specs=[VMEM, VMEM],
        out_shape=[
            jax.ShapeDtypeStruct((1, CHUNK, BLOCK), BF16),
            jax.ShapeDtypeStruct((8, CHUNK, BLOCK), BF16),
        ],
        name="sum_and_copy",
        cost_estimate=pl.CostEstimate(flops=1 << 18, bytes_accessed=1 << 20, transcendentals=0),
    )(parts)


def after(value, *others):
    return lax.optimization_barrier((value, *others))[0]


def spread(rows):
    whole = exchange(jnp.broadcast_to(rows[None], (8, CHUNK, BLOCK)), HOLDERS)
    return whole.reshape(LOCAL * BLOCK, BLOCK)


def shards(wave, left_ops, right_ops, site_ops, reach, pairing, site_tensor):
    pair = pairing[0]
    me = lax.axis_index("op")
    place = jnp.stack([me >> 4, (me >> 1) & 3, me & 1]).astype(jnp.int32)

    own_rows = lax.ppermute(wave[0], "op", TO_HOLDERS)
    renewed_kept = renew(True, place, pair, left_ops, site_tensor)
    field = spread(after(own_rows, renewed_kept))
    kept, *passed = pack(
        after(place, renewed_kept, own_rows),
        pair,
        site_ops.reshape(-1),
        reach[0],
        left_ops,
        right_ops,
    )
    kept, *passed, renewed_kept, later, field = lax.optimization_barrier(
        (kept, *passed, renewed_kept, place, field)
    )
    kept = exchange(kept, LINES)
    passed = [lax.ppermute(passed[d], "op", along(d, 1)) for d in (1, 2, 3, 0)]
    renewed_passed = renew(False, later, pair, left_ops, site_tensor)
    near, far = [
        lax.ppermute(value, "sect", [(0, 1), (1, 0)]).reshape(4, STACK, BLOCK)
        for value in (renewed_kept, renewed_passed)
    ]
    near = [lax.ppermute(near[d], "op", along(d, 0)) for d in (1, 2, 3)] + [near[0]]
    far = [lax.ppermute(far[d], "op", along(d, 1)) for d in (1, 2, 3, 0)]

    partial = apply_terms(place, field, [kept, *passed])
    half = apply_terms(place, field, [kept], near, kind=F32)
    parts = exchange(after(partial, *near).reshape(8, 1, CHUNK, BLOCK), HOLDERS)
    parts, half = lax.optimization_barrier((parts, half))
    first, copies = sum_and_copy(parts)
    first_field = exchange(copies, HOLDERS).reshape(LOCAL * BLOCK, BLOCK)
    partial = apply_terms(place, first_field, [kept, *passed])
    partial = apply_terms(place, after(field, partial), passed, far, half, partial)
    images = jnp.concatenate([first, reduce_chunks(partial)])
    images = lax.ppermute(images, "op", TO_OWNERS)
    return images[0:1], images[1:2], images[2:3]


def solution(mesh):
    placed = (
        P("sect", "op", None),
        P("sect", "op", None, None, None),
        P("sect", "op", None, None, None),
        P("sect", "op", None, None),
        P("sect", "op"),
        P("sect", None),
        P("sect", None, None, None, None),
    )
    return jax.shard_map(
        shards,
        mesh=mesh,
        in_specs=placed,
        out_specs=(P("sect", "op", None), P("sect", "op", None), P("sect", "op", None)),
        check_vma=False,
    )
```
